256 devices in a mesh: dp: 16 (over x, y), expert: 16 (over z, core).
Axes of the slice: x: 4, y: 4, z: 8, core: 2. Of those that a mesh axis runs over, the one named last changes fastest.
Arguments:
- tokens: bfloat16 [262144, 2048], P(('dp', 'expert')), may hold values from -16 to 16
- slot_param: bfloat16 [2048, 128], replicated, may hold values from -10 to 10
- pattern: int32 [128, 2048], P(None, ('dp', 'expert')), may hold values from 0 to 1, as said below
- w_in: bfloat16 [32, 2048, 4096], P('expert', None, 'dp'), may hold values from -0.125 to 0.125
- w_out: bfloat16 [32, 4096, 2048], P('expert', 'dp'), may hold values from -0.09375 to 0.09375
Outputs:
- mixed: bfloat16 [262144, 2048], P(('dp', 'expert'))
The draws below stay inside these ranges and needn't reach their ends.
Inputs may be any that keep to these rules, and one draw needn't show every extreme that they name: `pattern`: every slot sees at least one block; about a quarter of all pairs are 1.
All inputs are finite; a program needn't handle non-finite values.
Results may differ from the reference program's by a relative error of at most 0.0095.
Values may be sent and summed in bfloat16 or wider, within the bound.
No kernel may reach another device: no remote copies, remote signals or barrier semaphores. Data moves between devices by JAX's collectives and lax.ppermute only.
A program may use at most 64 MiB of HBM per device.

```python
import math
import jax
import jax.numpy as jnp
from jax import lax

D = 2048
H = 4096
SLOTS = 4
BLOCK = 128
EXPERTS = 32
TOKENS = 262144


def forced_blocks(key):
    return jax.random.randint(jax.random.fold_in(key, 7), (EXPERTS * SLOTS,), 0, TOKENS // BLOCK)


def draw_pattern(key, part):
    nblocks = TOKENS // BLOCK
    picks = jax.random.randint(jax.random.fold_in(key, 3), (EXPERTS * SLOTS, nblocks), 0, 4)
    base = (picks == 0).astype(jnp.int32)
    forced = forced_blocks(key)
    marked = (jnp.arange(nblocks)[None, :] == forced[:, None]).astype(jnp.int32)
    return jnp.maximum(base, marked)


def draw_tokens(key, part):
    return jnp.clip(jax.random.normal(jax.random.fold_in(key, 17), (TOKENS, D), jnp.float32), -6.0, 6.0).astype(jnp.bfloat16)


def draw_slot_param(key, part):
    width = EXPERTS * SLOTS
    scale = 3.0 / math.sqrt(D)
    return (jnp.clip(jax.random.normal(jax.random.fold_in(key, 23), (D, width), jnp.float32), -6.0, 6.0) * scale).astype(jnp.bfloat16)


def level_of(own_key, shape, cuts, low, top_value):
    def one(position, parts):
        steps = jax.random.uniform(jax.random.fold_in(jax.random.fold_in(own_key, 6), position), (parts,), jnp.float32, low / len(cuts), top_value / len(cuts))
        return jnp.repeat(jnp.exp(steps), shape[position] // parts).reshape((-1,) + (1,) * (len(shape) - position - 1))

    loudness = one(*cuts[0])
    for cut in cuts[1:]:
        loudness = loudness * one(*cut)
    return loudness


def scatter_about(stream_key, shape, scale, reach, pieces=(), kind=jnp.bfloat16):
    drawn = jax.random.normal(stream_key, shape, jnp.float32) * scale
    if len(pieces) > 0:
        drawn = level_of(stream_key, shape, pieces, -0.22, 0.18) * drawn
    return jnp.clip(drawn, min=-reach, max=reach).astype(kind)


def setup_inputs(seed: int = 0) -> dict:
    splits = jax.random.split(jax.random.key(seed), 6)
    return {
        "tokens": draw_tokens(jax.random.fold_in(splits[5], 71), 0),
        "slot_param": draw_slot_param(jax.random.fold_in(splits[5], 71), 0),
        "pattern": draw_pattern(jax.random.fold_in(splits[5], 71), 0),
        "w_in": scatter_about(splits[3], (EXPERTS, D, H), D ** -0.5, 0.125, ((0, 16), (2, 16))),
        "w_out": scatter_about(splits[4], (EXPERTS, H, D), H ** -0.5, 0.09375, ((0, 16), (1, 16))),
    }


floor_value = -1e30


def reference(tokens, slot_param, pattern, w_in, w_out):
    logits = jnp.dot(tokens, slot_param, preferred_element_type=jnp.float32)
    visible = jnp.repeat(pattern.T > 0, BLOCK, axis=0)
    slot_peak = jnp.max(jnp.where(visible, logits, floor_value), axis=0)
    weights = jnp.where(visible, jnp.exp(logits - slot_peak[None, :]), 0.0).astype(jnp.bfloat16)
    weight_sum = jnp.sum(weights.astype(jnp.float32), axis=0)
    numerator = lax.dot_general(weights, tokens, (((0,), (0,)), ((), ())), preferred_element_type=jnp.float32)
    slot_in = (numerator / weight_sum[:, None]).astype(jnp.bfloat16)
    grouped = slot_in.reshape(EXPERTS, SLOTS, D)

    def expert_mlp(inputs):
        rows, first, second = inputs
        hidden = jax.nn.gelu(jnp.dot(rows, first, preferred_element_type=jnp.float32)).astype(jnp.bfloat16)
        return jnp.dot(hidden, second, preferred_element_type=jnp.float32).astype(jnp.bfloat16)

    slot_out = lax.map(expert_mlp, (grouped, w_in, w_out)).reshape(EXPERTS * SLOTS, D)
    mixing = jax.nn.softmax(logits, axis=1).astype(jnp.bfloat16)
    block_rows = 4096 if TOKENS % 4096 == 0 else TOKENS
    blocked = mixing.reshape(TOKENS // block_rows, block_rows, EXPERTS * SLOTS)

    def combine(piece):
        return jnp.dot(piece, slot_out, preferred_element_type=jnp.float32).astype(jnp.bfloat16)

    return lax.map(combine, blocked).reshape(TOKENS, D)
```

```python
import functools

import jax
import jax.numpy as jnp
from jax import lax
from jax.experimental import pallas as pl
from jax.experimental.pallas import tpu as pltpu
from jax.sharding import PartitionSpec as P

SLOTS = 4
BLOCK = 128
ROWS = 8
EXTRA = 128
FLOOR = -1e30

f32 = jnp.float32
bf16 = jnp.bfloat16


VMEM = pl.BlockSpec(memory_space=pltpu.VMEM)


def terms_of(x):
    high = x.astype(bf16).astype(f32)
    rest = x - high
    mid = rest.astype(bf16).astype(f32)
    return high, mid, (rest - mid).astype(bf16).astype(f32)


def extra_of(peak, total):
    rows = peak.shape[0]
    lane = lax.broadcasted_iota(jnp.int32, (rows, EXTRA), 1)
    tile = jnp.zeros((rows, EXTRA), f32)
    for at, term in enumerate(terms_of(peak) + terms_of(total)):
        tile = jnp.where(lane == at, term, tile)
    return tile.astype(bf16)


def columns_of(tile):
    tile = tile.astype(f32)
    peak = (tile[:, 0:1] + tile[:, 1:2]) + tile[:, 2:3]
    total = (tile[:, 3:4] + tile[:, 4:5]) + tile[:, 5:6]
    return peak, total


def merge(pieces, width):
    stats = [columns_of(piece[:, width:]) for piece in pieces]
    peak = functools.reduce(jnp.maximum, [s[0] for s in stats])
    scales = [jnp.exp(s[0] - peak) for s in stats]
    total = sum(scale * s[1] for scale, s in zip(scales, stats))
    number = sum(scale * piece[:, :width].astype(f32) for scale, piece in zip(scales, pieces))
    return number, peak, total


def dispatch_kernel(half, tokens_hbm, param_ref, pattern_ref, logits_ref, keep_ref, send_ref, tok, trans, wts, sems):
    count, width = tok.shape
    slots = param_ref.shape[1]
    chunks = sems.shape[0]
    step = count // chunks
    copies = [
        pltpu.make_async_copy(tokens_hbm.at[pl.ds(i * step, step)], tok.at[pl.ds(i * step, step)], sems.at[i])
        for i in range(chunks)
    ]
    for copy in copies:
        copy.start()
    core = lax.rem(lax.axis_index("expert"), 2)

    def source(k):
        side = jnp.where(k < half, core, 1 - core)
        k = jnp.where(k < half, k, k - half)
        return 2 * ROWS * (k // ROWS) + ROWS * side + k % ROWS

    square = (slots, slots)
    from_old = lax.broadcasted_iota(jnp.int32, square, 0) == source(lax.broadcasted_iota(jnp.int32, square, 1))
    to_new = lax.broadcasted_iota(jnp.int32, square, 1) == source(lax.broadcasted_iota(jnp.int32, square, 0))
    param = jnp.dot(param_ref[...], from_old.astype(f32).astype(bf16), preferred_element_type=f32).astype(bf16)
    seen = jnp.dot(
        to_new.astype(f32).astype(bf16), pattern_ref[...].astype(f32).astype(bf16), preferred_element_type=f32
    )
    peak = jnp.full((slots, BLOCK), FLOOR, f32)
    for i in range(chunks):
        copies[i].wait()
        logits = jnp.dot(tok[i * step : (i + 1) * step, :], param, preferred_element_type=f32)
        logits_ref[i * step : (i + 1) * step, :] = logits
        turned = logits.T
        trans[:, i * step : (i + 1) * step] = turned
        for j in range(step // BLOCK):
            b = i * (step // BLOCK) + j
            peak = jnp.maximum(
                peak, jnp.where(seen[:, b : b + 1] > 0.5, turned[:, j * BLOCK : (j + 1) * BLOCK], FLOOR)
            )
    peak = jnp.max(peak, axis=1, keepdims=True)
    total = jnp.zeros((slots, BLOCK), f32)
    for b in range(count // BLOCK):
        at = slice(b * BLOCK, (b + 1) * BLOCK)
        w = jnp.where(seen[:, b : b + 1] > 0.5, jnp.exp(trans[:, at] - peak), 0.0).astype(bf16)
        wts[:, at] = w
        total = total + w.astype(f32)
    total = jnp.sum(total, axis=1, keepdims=True)
    extra = extra_of(peak, total)
    keep_ref[:, width:] = extra[:half]
    send_ref[:, width:] = extra[half:]
    number = jnp.dot(wts[...], tok[...], preferred_element_type=f32)
    keep_ref[:, :width] = number[:half].astype(bf16)
    send_ref[:, :width] = number[half:].astype(bf16)


def dispatch(tokens, slot_param, pattern):
    count, width = tokens.shape
    slots = slot_param.shape[1]
    half = slots // 2
    packed = jax.ShapeDtypeStruct((half, width + EXTRA), bf16)
    chunks = 4
    return pl.pallas_call(
        functools.partial(dispatch_kernel, half),
        out_shape=(jax.ShapeDtypeStruct((count, slots), f32), packed, packed),
        in_specs=[pl.BlockSpec(memory_space=pl.ANY), VMEM, VMEM],
        out_specs=(VMEM, VMEM, VMEM),
        scratch_shapes=[
            pltpu.VMEM((count, width), bf16),
            pltpu.VMEM((slots, count), f32),
            pltpu.VMEM((slots, count), bf16),
            pltpu.SemaphoreType.DMA((chunks,)),
        ],
        compiler_params=pltpu.CompilerParams(vmem_limit_bytes=24 << 20),
        cost_estimate=pl.CostEstimate(
            flops=4 * count * width * slots, bytes_accessed=2 * count * width, transcendentals=count * slots
        ),
        name="dispatch",
    )(tokens, slot_param, pattern)


def mixing_kernel(logits_ref, out_ref):
    x = logits_ref[...]
    x = jnp.exp(x - jnp.max(x, axis=1, keepdims=True))
    out_ref[...] = (x / jnp.sum(x, axis=1, keepdims=True)).astype(bf16)


def mixing_of(logits):
    return pl.pallas_call(
        mixing_kernel,
        out_shape=jax.ShapeDtypeStruct(logits.shape, bf16),
        in_specs=[VMEM],
        out_specs=VMEM,
        compiler_params=pltpu.CompilerParams(vmem_limit_bytes=8 << 20),
        cost_estimate=pl.CostEstimate(
            flops=4 * logits.size, bytes_accessed=6 * logits.size, transcendentals=logits.size
        ),
        name="mixing",
    )(logits)


def pair_kernel(a_ref, b_ref, out_ref):
    width = out_ref.shape[1] - EXTRA
    number, peak, total = merge([a_ref, b_ref], width)
    out_ref[:, :width] = number.astype(bf16)
    out_ref[:, width:] = extra_of(peak, total)


def pair_merge(a, b):
    return pl.pallas_call(
        pair_kernel,
        out_shape=jax.ShapeDtypeStruct(a.shape, bf16),
        in_specs=[VMEM, VMEM],
        out_specs=VMEM,
        compiler_params=pltpu.CompilerParams(vmem_limit_bytes=8 << 20),
        name="pair_merge",
    )(a, b)


def spread_kernel(in_ref, out_ref):
    width = out_ref.shape[2] - EXTRA
    number, peak, total = merge([in_ref.at[i] for i in range(in_ref.shape[0])], width)
    number = number.astype(bf16)
    extra = extra_of(peak, total)
    for i in range(out_ref.shape[0]):
        out_ref[i, :, :width] = number
        out_ref[i, :, width:] = extra


def merge_and_spread(pieces, copies):
    return pl.pallas_call(
        spread_kernel,
        out_shape=jax.ShapeDtypeStruct((copies,) + pieces.shape[1:], bf16),
        in_specs=[VMEM],
        out_specs=VMEM,
        compiler_params=pltpu.CompilerParams(vmem_limit_bytes=8 << 20),
        name="merge_spread",
    )(pieces)


def mlp_kernel(in_ref, first_ref, second_ref, out_ref):
    width = in_ref.shape[2] - EXTRA
    number, _, total = merge([in_ref.at[i] for i in range(in_ref.shape[0])], width)
    slot_in = (number / total).astype(bf16)
    experts, hidden_width = second_ref.shape[0], second_ref.shape[1]
    value = jnp.zeros((ROWS, width), f32)
    for e in range(experts):
        x = jnp.dot(slot_in, first_ref[e], preferred_element_type=f32)
        x = jax.nn.gelu(x)
        owner = lax.broadcasted_iota(jnp.int32, (ROWS, hidden_width), 0) // SLOTS
        x = jnp.where(owner == e, x, 0.0).astype(bf16)
        value = value + jnp.dot(x, second_ref[e], preferred_element_type=f32)
    value = value.astype(bf16)
    for i in range(out_ref.shape[0]):
        out_ref[i] = value


def mlp(pieces, w_in, w_out):
    width = w_out.shape[2]
    return pl.pallas_call(
        mlp_kernel,
        out_shape=jax.ShapeDtypeStruct((pieces.shape[0], ROWS, width), bf16),
        in_specs=[VMEM, VMEM, VMEM],
        out_specs=VMEM,
        compiler_params=pltpu.CompilerParams(vmem_limit_bytes=24 << 20),
        name="mlp",
    )(pieces, w_in, w_out)


def sum_kernel(in_ref, out_ref):
    value = sum(in_ref[i].astype(f32) for i in range(in_ref.shape[0])).astype(bf16)
    for i in range(out_ref.shape[0]):
        out_ref[i] = value


def sum_and_spread(pieces, copies):
    return pl.pallas_call(
        sum_kernel,
        out_shape=jax.ShapeDtypeStruct((copies,) + pieces.shape[1:], bf16),
        in_specs=[VMEM],
        out_specs=VMEM,
        compiler_params=pltpu.CompilerParams(vmem_limit_bytes=8 << 20),
        name="sum_spread",
    )(pieces)


def combine_kernel(mixing_ref, own_ref, other_ref, out_ref, both):
    half = own_ref.shape[0]

    @pl.when(pl.program_id(0) == 0)
    def _():
        both[:half] = own_ref[...]
        both[half:] = other_ref[...]

    out_ref[...] = jnp.dot(mixing_ref[...], both[...], preferred_element_type=f32).astype(bf16)


def combine(mixing, own, other):
    count, slots = mixing.shape
    half, width = own.shape
    step = 256
    whole = pl.BlockSpec((half, width), lambda i: (0, 0))
    return pl.pallas_call(
        combine_kernel,
        grid=(count // step,),
        out_shape=jax.ShapeDtypeStruct((count, width), bf16),
        in_specs=[pl.BlockSpec((step, slots), lambda i: (i, 0)), whole, whole],
        out_specs=pl.BlockSpec((step, width), lambda i: (i, 0)),
        scratch_shapes=[pltpu.VMEM((slots, width), bf16)],
        compiler_params=pltpu.CompilerParams(vmem_limit_bytes=24 << 20),
        name="combine",
    )(mixing, own, other)


def local(dp, expert, tokens, slot_param, pattern, w_in, w_out):
    width = tokens.shape[1]
    swap = [(i, i ^ 1) for i in range(expert)]
    along_z = [list(range(core, expert, 2)) for core in range(2)]
    chips = expert // 2
    to_all = functools.partial(lax.all_to_all, split_axis=0, concat_axis=0, tiled=True)
    logits, keep, send = dispatch(tokens, slot_param, pattern)
    got = lax.ppermute(send, "expert", swap)
    mixing = mixing_of(logits)
    pair = pair_merge(keep, got)
    pieces = to_all(pair.reshape(chips, ROWS, width + EXTRA), "expert", axis_index_groups=along_z)
    pieces = to_all(merge_and_spread(pieces, dp), "dp")
    partial = to_all(mlp(pieces, w_in, w_out), "dp")
    own = to_all(sum_and_spread(partial, chips), "expert", axis_index_groups=along_z)
    own = own.reshape(chips * ROWS, width)
    other = lax.ppermute(own, "expert", swap)
    return combine(mixing, own, other)


def solution(mesh):
    return jax.shard_map(
        functools.partial(local, mesh.shape["dp"], mesh.shape["expert"]),
        mesh=mesh,
        in_specs=(
            P(("dp", "expert"), None),
            P(),
            P(None, ("dp", "expert")),
            P("expert", None, "dp"),
            P("expert", "dp", None),
        ),
        out_specs=P(("dp", "expert"), None),
        check_vma=False,
    )
```

```python
import functools

import jax
import jax.numpy as jnp
from jax import lax
from jax.experimental import pallas as pl
from jax.experimental.pallas import tpu as pltpu
from jax.sharding import PartitionSpec as P

SLOTS = 4
BLOCK = 128
ROWS = 8
EXTRA = 128
FLOOR = -1e30

f32 = jnp.float32
bf16 = jnp.bfloat16


VMEM = pl.BlockSpec(memory_space=pltpu.VMEM)
HBM = pl.BlockSpec(memory_space=pltpu.HBM)


def terms_of(x):
    high = x.astype(bf16).astype(f32)
    rest = x - high
    mid = rest.astype(bf16).astype(f32)
    return high, mid, (rest - mid).astype(bf16).astype(f32)


def extra_of(peak, total):
    rows = peak.shape[0]
    lane = lax.broadcasted_iota(jnp.int32, (rows, EXTRA), 1)
    tile = jnp.zeros((rows, EXTRA), f32)
    for at, term in enumerate(terms_of(peak) + terms_of(total)):
        tile = jnp.where(lane == at, term, tile)
    return tile.astype(bf16)


def columns_of(tile):
    tile = tile.astype(f32)
    peak = (tile[:, 0:1] + tile[:, 1:2]) + tile[:, 2:3]
    total = (tile[:, 3:4] + tile[:, 4:5]) + tile[:, 5:6]
    return peak, total


def merge(pieces, width):
    stats = [columns_of(piece[:, width:]) for piece in pieces]
    peak = functools.reduce(jnp.maximum, [s[0] for s in stats])
    scales = [jnp.exp(s[0] - peak) for s in stats]
    total = sum(scale * s[1] for scale, s in zip(scales, stats))
    number = sum(scale * piece[:, :width].astype(f32) for scale, piece in zip(scales, pieces))
    return number, peak, total


def dispatch_kernel(
    half, tokens_hbm, param_hbm, pattern_ref, logits_ref, keep_ref, send_ref, tok, par, trans, wts, sems, par_sem
):
    count, width = tok.shape
    slots = par.shape[1]
    chunks = sems.shape[0]
    step = count // chunks
    first = pltpu.make_async_copy(param_hbm, par, par_sem)
    first.start()
    copies = [
        pltpu.make_async_copy(tokens_hbm.at[pl.ds(i * step, step)], tok.at[pl.ds(i * step, step)], sems.at[i])
        for i in range(chunks)
    ]
    for copy in copies:
        copy.start()
    core = lax.rem(lax.axis_index("expert"), 2)

    def source(k):
        side = jnp.where(k < half, core, 1 - core)
        k = jnp.where(k < half, k, k - half)
        return 2 * ROWS * (k // ROWS) + ROWS * side + k % ROWS

    square = (slots, slots)
    from_old = lax.broadcasted_iota(jnp.int32, square, 0) == source(lax.broadcasted_iota(jnp.int32, square, 1))
    to_new = lax.broadcasted_iota(jnp.int32, square, 1) == source(lax.broadcasted_iota(jnp.int32, square, 0))
    seen = lax.dot_general(
        to_new.astype(f32).astype(bf16),
        pattern_ref[...].astype(f32).astype(bf16),
        (((1,), (1,)), ((), ())),
        preferred_element_type=f32,
    )
    first.wait()
    param = jnp.dot(par[...], from_old.astype(f32).astype(bf16), preferred_element_type=f32).astype(bf16)
    peak = jnp.full((slots, BLOCK), FLOOR, f32)
    for i in range(chunks):
        copies[i].wait()
        logits = jnp.dot(tok[i * step : (i + 1) * step, :], param, preferred_element_type=f32)
        logits_ref[i * step : (i + 1) * step, :] = logits
        turned = logits.T
        trans[:, i * step : (i + 1) * step] = turned
        for j in range(step // BLOCK):
            b = i * (step // BLOCK) + j
            peak = jnp.maximum(
                peak, jnp.where(seen[:, b : b + 1] > 0.5, turned[:, j * BLOCK : (j + 1) * BLOCK], FLOOR)
            )
    peak = jnp.max(peak, axis=1, keepdims=True)
    total = jnp.zeros((slots, BLOCK), f32)
    for b in range(count // BLOCK):
        at = slice(b * BLOCK, (b + 1) * BLOCK)
        w = jnp.where(seen[:, b : b + 1] > 0.5, jnp.exp(trans[:, at] - peak), 0.0).astype(bf16)
        wts[:, at] = w
        total = total + w.astype(f32)
    total = jnp.sum(total, axis=1, keepdims=True)
    extra = extra_of(peak, total)
    keep_ref[:, width:] = extra[:half]
    send_ref[:, width:] = extra[half:]
    number = jnp.dot(wts[...], tok[...], preferred_element_type=f32)
    keep_ref[:, :width] = number[:half].astype(bf16)
    send_ref[:, :width] = number[half:].astype(bf16)


def dispatch(tokens, slot_param, pattern):
    count, width = tokens.shape
    slots = slot_param.shape[1]
    half = slots // 2
    packed = jax.ShapeDtypeStruct((half, width + EXTRA), bf16)
    chunks = 4
    return pl.pallas_call(
        functools.partial(dispatch_kernel, half),
        out_shape=(jax.ShapeDtypeStruct((count, slots), f32), packed, packed),
        in_specs=[HBM, HBM, VMEM],
        out_specs=(VMEM, VMEM, VMEM),
        scratch_shapes=[
            pltpu.VMEM((count, width), bf16),
            pltpu.VMEM((width, slots), bf16),
            pltpu.VMEM((slots, count), f32),
            pltpu.VMEM((slots, count), bf16),
            pltpu.SemaphoreType.DMA((chunks,)),
            pltpu.SemaphoreType.DMA,
        ],
        compiler_params=pltpu.CompilerParams(vmem_limit_bytes=105 << 19),
        cost_estimate=pl.CostEstimate(
            flops=4 * count * width * slots, bytes_accessed=2 * count * width, transcendentals=count * slots
        ),
        name="dispatch",
    )(tokens, slot_param, pattern.T)


def mixing_kernel(logits_ref, out_ref):
    x = logits_ref[...]
    x = jnp.exp(x - jnp.max(x, axis=1, keepdims=True))
    out_ref[...] = (x / jnp.sum(x, axis=1, keepdims=True)).astype(bf16)


def mixing_of(logits):
    return pl.pallas_call(
        mixing_kernel,
        out_shape=jax.ShapeDtypeStruct(logits.shape, bf16),
        in_specs=[VMEM],
        out_specs=VMEM,
        compiler_params=pltpu.CompilerParams(vmem_limit_bytes=8 << 20),
        cost_estimate=pl.CostEstimate(
            flops=4 * logits.size, bytes_accessed=6 * logits.size, transcendentals=logits.size
        ),
        name="mixing",
    )(logits)


def pair_kernel(a_ref, b_ref, out_ref):
    width = out_ref.shape[1] - EXTRA
    number, peak, total = merge([a_ref, b_ref], width)
    out_ref[:, :width] = number.astype(bf16)
    out_ref[:, width:] = extra_of(peak, total)


def pair_merge(a, b):
    return pl.pallas_call(
        pair_kernel,
        out_shape=jax.ShapeDtypeStruct(a.shape, bf16),
        in_specs=[VMEM, VMEM],
        out_specs=VMEM,
        compiler_params=pltpu.CompilerParams(vmem_limit_bytes=8 << 20),
        name="pair_merge",
    )(a, b)


def spread_kernel(in_ref, out_ref):
    width = out_ref.shape[2] - EXTRA
    number, peak, total = merge([in_ref.at[i] for i in range(in_ref.shape[0])], width)
    number = number.astype(bf16)
    extra = extra_of(peak, total)
    for i in range(out_ref.shape[0]):
        out_ref[i, :, :width] = number
        out_ref[i, :, width:] = extra


def merge_and_spread(pieces, copies):
    return pl.pallas_call(
        spread_kernel,
        out_shape=jax.ShapeDtypeStruct((copies,) + pieces.shape[1:], bf16),
        in_specs=[VMEM],
        out_specs=VMEM,
        compiler_params=pltpu.CompilerParams(vmem_limit_bytes=8 << 20),
        name="merge_spread",
    )(pieces)


def mlp_kernel(in_ref, first_ref, second_ref, out_ref):
    width = in_ref.shape[2] - EXTRA
    number, _, total = merge([in_ref.at[i] for i in range(in_ref.shape[0])], width)
    slot_in = (number / total).astype(bf16)
    experts, hidden_width = second_ref.shape[0], second_ref.shape[1]
    value = jnp.zeros((ROWS, width), f32)
    for e in range(experts):
        x = jnp.dot(slot_in, first_ref[e], preferred_element_type=f32)
        x = jax.nn.gelu(x)
        owner = lax.broadcasted_iota(jnp.int32, (ROWS, hidden_width), 0) // SLOTS
        x = jnp.where(owner == e, x, 0.0).astype(bf16)
        value = value + jnp.dot(x, second_ref[e], preferred_element_type=f32)
    value = value.astype(bf16)
    for i in range(out_ref.shape[0]):
        out_ref[i] = value


def mlp(pieces, w_in, w_out):
    width = w_out.shape[2]
    return pl.pallas_call(
        mlp_kernel,
        out_shape=jax.ShapeDtypeStruct((pieces.shape[0], ROWS, width), bf16),
        in_specs=[VMEM, VMEM, VMEM],
        out_specs=VMEM,
        compiler_params=pltpu.CompilerParams(vmem_limit_bytes=24 << 20),
        name="mlp",
    )(pieces, w_in, w_out)


def sum_kernel(in_ref, out_ref):
    value = sum(in_ref[i].astype(f32) for i in range(in_ref.shape[0])).astype(bf16)
    for i in range(out_ref.shape[0]):
        out_ref[i] = value


def sum_and_spread(pieces, copies):
    return pl.pallas_call(
        sum_kernel,
        out_shape=jax.ShapeDtypeStruct((copies,) + pieces.shape[1:], bf16),
        in_specs=[VMEM],
        out_specs=VMEM,
        compiler_params=pltpu.CompilerParams(vmem_limit_bytes=8 << 20),
        name="sum_spread",
    )(pieces)


def combine_kernel(mixing_ref, own_ref, other_ref, out_ref, both):
    half = own_ref.shape[0]

    @pl.when(pl.program_id(0) == 0)
    def _():
        both[:half] = own_ref[...]
        both[half:] = other_ref[...]

    out_ref[...] = jnp.dot(mixing_ref[...], both[...], preferred_element_type=f32).astype(bf16)


def combine(mixing, own, other):
    count, slots = mixing.shape
    half, width = own.shape
    step = 256
    whole = pl.BlockSpec((half, width), lambda i: (0, 0))
    return pl.pallas_call(
        combine_kernel,
        grid=(count // step,),
        out_shape=jax.ShapeDtypeStruct((count, width), bf16),
        in_specs=[pl.BlockSpec((step, slots), lambda i: (i, 0)), whole, whole],
        out_specs=pl.BlockSpec((step, width), lambda i: (i, 0)),
        scratch_shapes=[pltpu.VMEM((slots, width), bf16)],
        compiler_params=pltpu.CompilerParams(vmem_limit_bytes=24 << 20),
        name="combine",
    )(mixing, own, other)


def local(dp, expert, tokens, slot_param, pattern, w_in, w_out):
    width = tokens.shape[1]
    swap = [(i, i ^ 1) for i in range(expert)]
    along_z = [list(range(core, expert, 2)) for core in range(2)]
    chips = expert // 2
    to_all = functools.partial(lax.all_to_all, split_axis=0, concat_axis=0, tiled=True)
    logits, keep, send = dispatch(tokens, slot_param, pattern)
    got = lax.ppermute(send, "expert", swap)
    mixing = mixing_of(logits)
    pair = pair_merge(keep, got)
    pieces = to_all(pair.reshape(chips, ROWS, width + EXTRA), "expert", axis_index_groups=along_z)
    pieces = to_all(merge_and_spread(pieces, dp), "dp")
    partial = to_all(mlp(pieces, w_in, w_out), "dp")
    own = to_all(sum_and_spread(partial, chips), "expert", axis_index_groups=along_z)
    own = own.reshape(chips * ROWS, width)
    other = lax.ppermute(own, "expert", swap)
    return combine(mixing, own, other)


def solution(mesh):
    return jax.shard_map(
        functools.partial(local, mesh.shape["dp"], mesh.shape["expert"]),
        mesh=mesh,
        in_specs=(
            P(("dp", "expert"), None),
            P(),
            P(None, ("dp", "expert")),
            P("expert", None, "dp"),
            P("expert", "dp", None),
        ),
        out_specs=P(("dp", "expert"), None),
        check_vma=False,
    )
```

```python
import functools

import jax
import jax.numpy as jnp
from jax import lax
from jax.experimental import pallas as pl
from jax.experimental.pallas import tpu as pltpu
from jax.sharding import PartitionSpec as P

SLOTS = 4
BLOCK = 128
ROWS = 8
EXTRA = 128
FLOOR = -1e30
CHUNK = 256
AHEAD = 2

f32 = jnp.float32
bf16 = jnp.bfloat16


VMEM = pl.BlockSpec(memory_space=pltpu.VMEM)
HBM = pl.BlockSpec(memory_space=pltpu.HBM)
COVER = pl.CostEstimate(flops=10**10, bytes_accessed=20 << 20, transcendentals=0)


def terms_of(x):
    high = x.astype(bf16).astype(f32)
    rest = x - high
    mid = rest.astype(bf16).astype(f32)
    return high, mid, (rest - mid).astype(bf16).astype(f32)


def extra_of(peak, total):
    rows = peak.shape[0]
    lane = lax.broadcasted_iota(jnp.int32, (rows, EXTRA), 1)
    tile = jnp.zeros((rows, EXTRA), f32)
    for at, term in enumerate(terms_of(peak) + terms_of(total)):
        tile = jnp.where(lane == at, term, tile)
    return tile.astype(bf16)


def columns_of(tile):
    tile = tile.astype(f32)
    peak = (tile[:, 0:1] + tile[:, 1:2]) + tile[:, 2:3]
    total = (tile[:, 3:4] + tile[:, 4:5]) + tile[:, 5:6]
    return peak, total


def merge(pieces, width):
    stats = [columns_of(piece[:, width:]) for piece in pieces]
    peak = functools.reduce(jnp.maximum, [s[0] for s in stats])
    scales = [jnp.exp(s[0] - peak) for s in stats]
    total = sum(scale * s[1] for scale, s in zip(scales, stats))
    number = sum(scale * piece[:, :width].astype(f32) for scale, piece in zip(scales, pieces))
    return number, peak, total


def dispatch_kernel(
    half,
    chunks,
    tokens_hbm,
    param_hbm,
    pattern_hbm,
    turned_ref,
    keep_ref,
    send_ref,
    tok,
    par,
    pattern_ref,
    wts,
    sems,
    par_sem,
    pattern_sem,
):
    count, width = tok.shape
    slots = par.shape[1]
    first = pltpu.make_async_copy(param_hbm, par, par_sem)
    first.start()
    shown = pltpu.make_async_copy(pattern_hbm, pattern_ref, pattern_sem)
    shown.start()
    copies = [
        pltpu.make_async_copy(tokens_hbm.at[pl.ds(at, size)], tok.at[pl.ds(at, size)], sems.at[i])
        for i, (at, size) in enumerate(chunks)
    ]
    for copy in copies[:AHEAD]:
        copy.start()
    core = lax.rem(lax.axis_index("expert"), 2)

    def own_first(x):
        groups = [x[i : i + ROWS] for i in range(0, slots, ROWS)]
        own = [jnp.where(core == 0, low, high) for low, high in zip(groups[::2], groups[1::2])]
        other = [jnp.where(core == 0, high, low) for low, high in zip(groups[::2], groups[1::2])]
        return jnp.concatenate(own + other, axis=0)

    square = (slots, slots)
    same = lax.broadcasted_iota(jnp.int32, square, 0) == lax.broadcasted_iota(jnp.int32, square, 1)
    shown.wait()
    seen = own_first(
        lax.dot_general(
            same.astype(f32).astype(bf16),
            pattern_ref[...].astype(f32).astype(bf16),
            (((1,), (1,)), ((), ())),
            preferred_element_type=f32,
        )
    )
    first.wait()
    peak = jnp.full((slots, BLOCK), FLOOR, f32)
    for i, (at, size) in enumerate(chunks):
        copies[i].wait()
        if i + AHEAD < len(chunks):
            copies[i + AHEAD].start()
        turned = own_first(jnp.dot(tok[at : at + size, :], par[...], preferred_element_type=f32).T)
        turned_ref[:, at : at + size] = turned
        for j in range(0, size, BLOCK):
            b = (at + j) // BLOCK
            peak = jnp.maximum(peak, jnp.where(seen[:, b : b + 1] > 0.5, turned[:, j : j + BLOCK], FLOOR))
    peak = jnp.max(peak, axis=1, keepdims=True)
    total = jnp.zeros((slots, BLOCK), f32)
    for b in range(count // BLOCK):
        at = slice(b * BLOCK, (b + 1) * BLOCK)
        w = jnp.where(seen[:, b : b + 1] > 0.5, jnp.exp(turned_ref[:, at] - peak), 0.0).astype(bf16)
        wts[:, at] = w
        total = total + w.astype(f32)
    number = jnp.dot(wts[...], tok[...], preferred_element_type=f32)
    keep_ref[:, :width] = number[:half].astype(bf16)
    send_ref[:, :width] = number[half:].astype(bf16)
    extra = extra_of(peak, jnp.sum(total, axis=1, keepdims=True))
    keep_ref[:, width:] = extra[:half]
    send_ref[:, width:] = extra[half:]


def dispatch(tokens, slot_param, pattern):
    count, width = tokens.shape
    slots = slot_param.shape[1]
    half = slots // 2
    packed = pltpu.VMEM((half, width + EXTRA), bf16)
    chunks = [(at, CHUNK) for at in range(0, count, CHUNK)]
    return pl.pallas_call(
        functools.partial(dispatch_kernel, half, chunks),
        out_shape=(pltpu.VMEM((slots, count), f32), packed, packed),
        in_specs=[HBM, HBM, HBM],
        out_specs=(VMEM, VMEM, VMEM),
        scratch_shapes=[
            pltpu.VMEM((count, width), bf16),
            pltpu.VMEM((width, slots), bf16),
            pltpu.VMEM(pattern.shape[::-1], jnp.int32),
            pltpu.VMEM((slots, count), bf16),
            pltpu.SemaphoreType.DMA((len(chunks),)),
            pltpu.SemaphoreType.DMA,
            pltpu.SemaphoreType.DMA,
        ],
        compiler_params=pltpu.CompilerParams(vmem_limit_bytes=24 << 20),
        cost_estimate=pl.CostEstimate(
            flops=4 * count * width * slots, bytes_accessed=2 * count * width, transcendentals=count * slots
        ),
        name="dispatch",
    )(*(pltpu.with_memory_space_constraint(x, pltpu.HBM) for x in (tokens, slot_param, pattern.T)))


def mixing_kernel(turned_ref, out_ref):
    x = turned_ref[...]
    x = jnp.exp(x - jnp.max(x, axis=0, keepdims=True))
    out_ref[...] = (x / jnp.sum(x, axis=0, keepdims=True)).T.astype(bf16)


def mixing_of(turned):
    return pl.pallas_call(
        mixing_kernel,
        out_shape=jax.ShapeDtypeStruct(turned.shape[::-1], bf16),
        in_specs=[VMEM],
        out_specs=VMEM,
        compiler_params=pltpu.CompilerParams(vmem_limit_bytes=8 << 20),
        cost_estimate=pl.CostEstimate(
            flops=4 * turned.size, bytes_accessed=6 * turned.size, transcendentals=turned.size
        ),
        name="mixing",
    )(turned)


def pair_kernel(a_ref, b_ref, out_ref):
    width = out_ref.shape[1] - EXTRA
    number, peak, total = merge([a_ref, b_ref], width)
    out_ref[:, :width] = number.astype(bf16)
    out_ref[:, width:] = extra_of(peak, total)


def pair_merge(a, b):
    return pl.pallas_call(
        pair_kernel,
        out_shape=jax.ShapeDtypeStruct(a.shape, bf16),
        in_specs=[VMEM, VMEM],
        out_specs=VMEM,
        compiler_params=pltpu.CompilerParams(vmem_limit_bytes=8 << 20),
        cost_estimate=COVER,
        name="pair_merge",
    )(a, b)


def spread_kernel(in_ref, out_ref):
    width = out_ref.shape[2] - EXTRA
    number, peak, total = merge([in_ref.at[i] for i in range(in_ref.shape[0])], width)
    number = number.astype(bf16)
    extra = extra_of(peak, total)
    for i in range(out_ref.shape[0]):
        out_ref[i, :, :width] = number
        out_ref[i, :, width:] = extra


def merge_and_spread(pieces, copies):
    return pl.pallas_call(
        spread_kernel,
        out_shape=jax.ShapeDtypeStruct((copies,) + pieces.shape[1:], bf16),
        in_specs=[VMEM],
        out_specs=VMEM,
        compiler_params=pltpu.CompilerParams(vmem_limit_bytes=8 << 20),
        cost_estimate=COVER,
        name="merge_spread",
    )(pieces)


def mlp_kernel(in_ref, first_ref, second_ref, out_ref):
    width = in_ref.shape[2] - EXTRA
    number, _, total = merge([in_ref.at[i] for i in range(in_ref.shape[0])], width)
    slot_in = (number / total).astype(bf16)
    experts, hidden_width = second_ref.shape[0], second_ref.shape[1]
    value = jnp.zeros((ROWS, width), f32)
    for e in range(experts):
        x = jnp.dot(slot_in, first_ref[e], preferred_element_type=f32)
        x = jax.nn.gelu(x)
        owner = lax.broadcasted_iota(jnp.int32, (ROWS, hidden_width), 0) // SLOTS
        x = jnp.where(owner == e, x, 0.0).astype(bf16)
        value = value + jnp.dot(x, second_ref[e], preferred_element_type=f32)
    value = value.astype(bf16)
    for i in range(out_ref.shape[0]):
        out_ref[i] = value


def mlp(pieces, w_in, w_out):
    width = w_out.shape[2]
    return pl.pallas_call(
        mlp_kernel,
        out_shape=jax.ShapeDtypeStruct((pieces.shape[0], ROWS, width), bf16),
        in_specs=[VMEM, VMEM, VMEM],
        out_specs=VMEM,
        compiler_params=pltpu.CompilerParams(vmem_limit_bytes=24 << 20),
        name="mlp",
    )(pieces, w_in, w_out)


def sum_kernel(in_ref, out_ref):
    value = sum(in_ref[i].astype(f32) for i in range(in_ref.shape[0])).astype(bf16)
    for i in range(out_ref.shape[0]):
        out_ref[i] = value


def sum_and_spread(pieces, copies):
    return pl.pallas_call(
        sum_kernel,
        out_shape=jax.ShapeDtypeStruct((copies,) + pieces.shape[1:], bf16),
        in_specs=[VMEM],
        out_specs=VMEM,
        compiler_params=pltpu.CompilerParams(vmem_limit_bytes=8 << 20),
        name="sum_spread",
    )(pieces)


def combine_kernel(mixing_ref, own_ref, other_ref, out_hbm, both, rows, sems):
    half = own_ref.shape[0]
    both[:half] = own_ref[...]
    both[half:] = other_ref[...]
    step = rows.shape[0] // sems.shape[0]
    copies = []
    for i in range(sems.shape[0]):
        at = pl.ds(i * step, step)
        rows[at] = jnp.dot(mixing_ref[at], both[...], preferred_element_type=f32).astype(bf16)
        copies.append(pltpu.make_async_copy(rows.at[at], out_hbm.at[at], sems.at[i]))
        copies[-1].start()
    for copy in copies:
        copy.wait()


def combine(mixing, own, other):
    count, slots = mixing.shape
    width = own.shape[1]
    return pl.pallas_call(
        combine_kernel,
        out_shape=jax.ShapeDtypeStruct((count, width), bf16),
        in_specs=[VMEM, VMEM, VMEM],
        out_specs=HBM,
        scratch_shapes=[
            pltpu.VMEM((slots, width), bf16),
            pltpu.VMEM((count, width), bf16),
            pltpu.SemaphoreType.DMA((8,)),
        ],
        compiler_params=pltpu.CompilerParams(vmem_limit_bytes=24 << 20),
        name="combine",
    )(mixing, own, other)


def local(dp, expert, tokens, slot_param, pattern, w_in, w_out):
    width = tokens.shape[1]
    swap = [(i, i ^ 1) for i in range(expert)]
    along_z = [list(range(core, expert, 2)) for core in range(2)]
    chips = expert // 2
    to_all = functools.partial(lax.all_to_all, split_axis=0, concat_axis=0, tiled=True)
    turned, keep, send = dispatch(tokens, slot_param, pattern)
    got = lax.ppermute(send, "expert", swap)
    mixing = mixing_of(turned)
    pair = pair_merge(keep, got)
    pieces = to_all(pair.reshape(chips, ROWS, width + EXTRA), "expert", axis_index_groups=along_z)
    pieces = to_all(merge_and_spread(pieces, dp), "dp")
    partial = to_all(mlp(pieces, w_in, w_out), "dp")
    own = to_all(sum_and_spread(partial, chips), "expert", axis_index_groups=along_z)
    own = own.reshape(chips * ROWS, width)
    other = lax.ppermute(own, "expert", swap)
    return combine(mixing, own, other)


def solution(mesh):
    return jax.shard_map(
        functools.partial(local, mesh.shape["dp"], mesh.shape["expert"]),
        mesh=mesh,
        in_specs=(
            P(("dp", "expert"), None),
            P(),
            P(None, ("dp", "expert")),
            P("expert", None, "dp"),
            P("expert", "dp", None),
        ),
        out_specs=P(("dp", "expert"), None),
        check_vma=False,
    )
```

```python
import functools

import jax
import jax.numpy as jnp
from jax import lax
from jax.experimental import pallas as pl
from jax.experimental.pallas import tpu as pltpu
from jax.sharding import PartitionSpec as P

SLOTS = 4
BLOCK = 128
ROWS = 8
EXTRA = 128
FLOOR = -1e30
CHUNK = 256
AHEAD = 2

f32 = jnp.float32
bf16 = jnp.bfloat16


VMEM = pl.BlockSpec(memory_space=pltpu.VMEM)
HBM = pl.BlockSpec(memory_space=pltpu.HBM)
COVER = pl.CostEstimate(flops=10**10, bytes_accessed=20 << 20, transcendentals=0)


def terms_of(x):
    high = x.astype(bf16).astype(f32)
    rest = x - high
    mid = rest.astype(bf16).astype(f32)
    return high, mid, (rest - mid).astype(bf16).astype(f32)


def extra_of(peak, total):
    rows = peak.shape[0]
    lane = lax.broadcasted_iota(jnp.int32, (rows, EXTRA), 1)
    tile = jnp.zeros((rows, EXTRA), f32)
    for at, term in enumerate(terms_of(peak) + terms_of(total)):
        tile = jnp.where(lane == at, term, tile)
    return tile.astype(bf16)


def columns_of(tile):
    tile = tile.astype(f32)
    peak = (tile[:, 0:1] + tile[:, 1:2]) + tile[:, 2:3]
    total = (tile[:, 3:4] + tile[:, 4:5]) + tile[:, 5:6]
    return peak, total


def merge(pieces, width):
    stats = [columns_of(piece[:, width:]) for piece in pieces]
    peak = functools.reduce(jnp.maximum, [s[0] for s in stats])
    scales = [jnp.exp(s[0] - peak) for s in stats]
    total = sum(scale * s[1] for scale, s in zip(scales, stats))
    number = sum(scale * piece[:, :width].astype(f32) for scale, piece in zip(scales, pieces))
    return number, peak, total


def dispatch_kernel(
    half,
    chunks,
    tokens_hbm,
    param_hbm,
    pattern_hbm,
    turned_ref,
    keep_ref,
    send_ref,
    tok,
    par,
    pattern_ref,
    wts,
    number,
    sems,
    par_sem,
    pattern_sem,
):
    count, width = tok.shape
    slots = par.shape[1]
    first = pltpu.make_async_copy(param_hbm, par, par_sem)
    first.start()
    shown = pltpu.make_async_copy(pattern_hbm, pattern_ref, pattern_sem)
    shown.start()
    copies = [
        pltpu.make_async_copy(tokens_hbm.at[pl.ds(at, size)], tok.at[pl.ds(at, size)], sems.at[i])
        for i, (at, size) in enumerate(chunks)
    ]
    for copy in copies[:AHEAD]:
        copy.start()
    core = lax.rem(lax.axis_index("expert"), 2)

    def own_first(x):
        groups = [x[i : i + ROWS] for i in range(0, slots, ROWS)]
        own = [jnp.where(core == 0, low, high) for low, high in zip(groups[::2], groups[1::2])]
        other = [jnp.where(core == 0, high, low) for low, high in zip(groups[::2], groups[1::2])]
        return jnp.concatenate(own + other, axis=0)

    square = (slots, slots)
    same = lax.broadcasted_iota(jnp.int32, square, 0) == lax.broadcasted_iota(jnp.int32, square, 1)
    shown.wait()
    seen = own_first(
        lax.dot_general(
            same.astype(f32).astype(bf16),
            pattern_ref[...].astype(f32).astype(bf16),
            (((1,), (1,)), ((), ())),
            preferred_element_type=f32,
        )
    )
    first.wait()
    peak = jnp.full((slots, 1), FLOOR, f32)
    total = jnp.zeros((slots, BLOCK), f32)
    for i, (at, size) in enumerate(chunks):
        copies[i].wait()
        if i + AHEAD < len(chunks):
            copies[i + AHEAD].start()
        turned = own_first(jnp.dot(tok[at : at + size, :], par[...], preferred_element_type=f32).T)
        turned_ref[:, at : at + size] = turned
        blocks = []
        for j in range(0, size, BLOCK):
            b = (at + j) // BLOCK
            blocks.append((seen[:, b : b + 1] > 0.5, turned[:, j : j + BLOCK]))
        before = peak
        top = functools.reduce(jnp.maximum, [jnp.where(shows, x, FLOOR) for shows, x in blocks])
        peak = jnp.maximum(peak, jnp.max(top, axis=1, keepdims=True))
        scale = jnp.exp(before - peak)
        total = total * scale
        for j, (shows, x) in enumerate(blocks):
            w = jnp.where(shows, jnp.exp(x - peak), 0.0).astype(bf16)
            wts[:, at + j * BLOCK : at + (j + 1) * BLOCK] = w
            total = total + w.astype(f32)
        if i == 1:
            number[...] = jnp.dot(wts[:, :at], tok[:at], preferred_element_type=f32) * scale
        elif i > 1:
            last = slice(chunks[i - 1][0], at)
            number[...] = (number[...] + jnp.dot(wts[:, last], tok[last], preferred_element_type=f32)) * scale
    last = slice(chunks[-1][0], count)
    result = number[...] + jnp.dot(wts[:, last], tok[last], preferred_element_type=f32)
    keep_ref[:, :width] = result[:half].astype(bf16)
    send_ref[:, :width] = result[half:].astype(bf16)
    extra = extra_of(peak, jnp.sum(total, axis=1, keepdims=True))
    keep_ref[:, width:] = extra[:half]
    send_ref[:, width:] = extra[half:]


def dispatch(tokens, slot_param, pattern):
    count, width = tokens.shape
    slots = slot_param.shape[1]
    half = slots // 2
    packed = pltpu.VMEM((half, width + EXTRA), bf16)
    chunks = [(at, CHUNK) for at in range(0, count, CHUNK)]
    return pl.pallas_call(
        functools.partial(dispatch_kernel, half, chunks),
        out_shape=(pltpu.VMEM((slots, count), f32), packed, packed),
        in_specs=[HBM, HBM, HBM],
        out_specs=(VMEM, VMEM, VMEM),
        scratch_shapes=[
            pltpu.VMEM((count, width), bf16),
            pltpu.VMEM((width, slots), bf16),
            pltpu.VMEM(pattern.shape[::-1], jnp.int32),
            pltpu.VMEM((slots, count), bf16),
            pltpu.VMEM((slots, width), f32),
            pltpu.SemaphoreType.DMA((len(chunks),)),
            pltpu.SemaphoreType.DMA,
            pltpu.SemaphoreType.DMA,
        ],
        compiler_params=pltpu.CompilerParams(vmem_limit_bytes=24 << 20),
        cost_estimate=pl.CostEstimate(
            flops=4 * count * width * slots, bytes_accessed=2 * count * width, transcendentals=count * slots
        ),
        name="dispatch",
    )(*(pltpu.with_memory_space_constraint(x, pltpu.HBM) for x in (tokens, slot_param, pattern.T)))


def mixing_kernel(turned_ref, out_ref):
    x = turned_ref[...]
    x = jnp.exp(x - jnp.max(x, axis=0, keepdims=True))
    out_ref[...] = (x / jnp.sum(x, axis=0, keepdims=True)).T.astype(bf16)


def mixing_of(turned):
    return pl.pallas_call(
        mixing_kernel,
        out_shape=jax.ShapeDtypeStruct(turned.shape[::-1], bf16),
        in_specs=[VMEM],
        out_specs=VMEM,
        compiler_params=pltpu.CompilerParams(vmem_limit_bytes=8 << 20),
        cost_estimate=pl.CostEstimate(
            flops=4 * turned.size, bytes_accessed=6 * turned.size, transcendentals=turned.size
        ),
        name="mixing",
    )(turned)


def pair_kernel(a_ref, b_ref, out_ref):
    width = out_ref.shape[1] - EXTRA
    number, peak, total = merge([a_ref, b_ref], width)
    out_ref[:, :width] = number.astype(bf16)
    out_ref[:, width:] = extra_of(peak, total)


def pair_merge(a, b):
    return pl.pallas_call(
        pair_kernel,
        out_shape=jax.ShapeDtypeStruct(a.shape, bf16),
        in_specs=[VMEM, VMEM],
        out_specs=VMEM,
        compiler_params=pltpu.CompilerParams(vmem_limit_bytes=8 << 20),
        cost_estimate=COVER,
        name="pair_merge",
    )(a, b)


def spread_kernel(in_ref, out_ref):
    width = out_ref.shape[2] - EXTRA
    number, peak, total = merge([in_ref.at[i] for i in range(in_ref.shape[0])], width)
    number = number.astype(bf16)
    extra = extra_of(peak, total)
    for i in range(out_ref.shape[0]):
        out_ref[i, :, :width] = number
        out_ref[i, :, width:] = extra


def merge_and_spread(pieces, copies):
    return pl.pallas_call(
        spread_kernel,
        out_shape=jax.ShapeDtypeStruct((copies,) + pieces.shape[1:], bf16),
        in_specs=[VMEM],
        out_specs=VMEM,
        compiler_params=pltpu.CompilerParams(vmem_limit_bytes=8 << 20),
        cost_estimate=COVER,
        name="merge_spread",
    )(pieces)


def mlp_kernel(in_ref, first_ref, second_ref, out_ref):
    width = in_ref.shape[2] - EXTRA
    number, _, total = merge([in_ref.at[i] for i in range(in_ref.shape[0])], width)
    slot_in = (number / total).astype(bf16)
    experts, hidden_width = second_ref.shape[0], second_ref.shape[1]
    value = jnp.zeros((ROWS, width), f32)
    for e in range(experts):
        x = jnp.dot(slot_in, first_ref[e], preferred_element_type=f32)
        x = jax.nn.gelu(x)
        owner = lax.broadcasted_iota(jnp.int32, (ROWS, hidden_width), 0) // SLOTS
        x = jnp.where(owner == e, x, 0.0).astype(bf16)
        value = value + jnp.dot(x, second_ref[e], preferred_element_type=f32)
    value = value.astype(bf16)
    for i in range(out_ref.shape[0]):
        out_ref[i] = value


def mlp(pieces, w_in, w_out):
    width = w_out.shape[2]
    return pl.pallas_call(
        mlp_kernel,
        out_shape=jax.ShapeDtypeStruct((pieces.shape[0], ROWS, width), bf16),
        in_specs=[VMEM, VMEM, VMEM],
        out_specs=VMEM,
        compiler_params=pltpu.CompilerParams(vmem_limit_bytes=24 << 20),
        name="mlp",
    )(pieces, w_in, w_out)


def sum_kernel(in_ref, out_ref):
    value = sum(in_ref[i].astype(f32) for i in range(in_ref.shape[0])).astype(bf16)
    for i in range(out_ref.shape[0]):
        out_ref[i] = value


def sum_and_spread(pieces, copies):
    return pl.pallas_call(
        sum_kernel,
        out_shape=jax.ShapeDtypeStruct((copies,) + pieces.shape[1:], bf16),
        in_specs=[VMEM],
        out_specs=VMEM,
        compiler_params=pltpu.CompilerParams(vmem_limit_bytes=8 << 20),
        name="sum_spread",
    )(pieces)


def combine_kernel(mixing_ref, own_ref, other_ref, out_hbm, both, rows, sems):
    half = own_ref.shape[0]
    both[:half] = own_ref[...]
    both[half:] = other_ref[...]
    step = rows.shape[0] // sems.shape[0]
    copies = []
    for i in range(sems.shape[0]):
        at = pl.ds(i * step, step)
        rows[at] = jnp.dot(mixing_ref[at], both[...], preferred_element_type=f32).astype(bf16)
        copies.append(pltpu.make_async_copy(rows.at[at], out_hbm.at[at], sems.at[i]))
        copies[-1].start()
    for copy in copies:
        copy.wait()


def combine(mixing, own, other):
    count, slots = mixing.shape
    width = own.shape[1]
    return pl.pallas_call(
        combine_kernel,
        out_shape=jax.ShapeDtypeStruct((count, width), bf16),
        in_specs=[VMEM, VMEM, VMEM],
        out_specs=HBM,
        scratch_shapes=[
            pltpu.VMEM((slots, width), bf16),
            pltpu.VMEM((count, width), bf16),
            pltpu.SemaphoreType.DMA((8,)),
        ],
        compiler_params=pltpu.CompilerParams(vmem_limit_bytes=24 << 20),
        name="combine",
    )(mixing, own, other)


def local(dp, expert, tokens, slot_param, pattern, w_in, w_out):
    width = tokens.shape[1]
    swap = [(i, i ^ 1) for i in range(expert)]
    along_z = [list(range(core, expert, 2)) for core in range(2)]
    chips = expert // 2
    to_all = functools.partial(lax.all_to_all, split_axis=0, concat_axis=0, tiled=True)
    turned, keep, send = dispatch(tokens, slot_param, pattern)
    got = lax.ppermute(send, "expert", swap)
    mixing = mixing_of(turned)
    pair = pair_merge(keep, got)
    pieces = to_all(pair.reshape(chips, ROWS, width + EXTRA), "expert", axis_index_groups=along_z)
    pieces = to_all(merge_and_spread(pieces, dp), "dp")
    partial = to_all(mlp(pieces, w_in, w_out), "dp")
    own = to_all(sum_and_spread(partial, chips), "expert", axis_index_groups=along_z)
    own = own.reshape(chips * ROWS, width)
    other = lax.ppermute(own, "expert", swap)
    return combine(mixing, own, other)


def solution(mesh):
    return jax.shard_map(
        functools.partial(local, mesh.shape["dp"], mesh.shape["expert"]),
        mesh=mesh,
        in_specs=(
            P(("dp", "expert"), None),
            P(),
            P(None, ("dp", "expert")),
            P("expert", None, "dp"),
            P("expert", "dp", None),
        ),
        out_specs=P(("dp", "expert"), None),
        check_vma=False,
    )
```

```python
import functools

import jax
import jax.numpy as jnp
from jax import lax
from jax.experimental import pallas as pl
from jax.experimental.pallas import tpu as pltpu
from jax.sharding import PartitionSpec as P

SLOTS = 4
BLOCK = 128
ROWS = 8
EXTRA = 128
FLOOR = -1e30
CHUNK = 256
AHEAD = 2

f32 = jnp.float32
bf16 = jnp.bfloat16


VMEM = pl.BlockSpec(memory_space=pltpu.VMEM)
HBM = pl.BlockSpec(memory_space=pltpu.HBM)


def terms_of(x):
    high = x.astype(bf16).astype(f32)
    rest = x - high
    mid = rest.astype(bf16).astype(f32)
    return high, mid, (rest - mid).astype(bf16).astype(f32)


def extra_of(peak, total):
    rows = peak.shape[0]
    lane = lax.broadcasted_iota(jnp.int32, (rows, EXTRA), 1)
    tile = jnp.zeros((rows, EXTRA), f32)
    for at, term in enumerate(terms_of(peak) + terms_of(total)):
        tile = jnp.where(lane == at, term, tile)
    return tile.astype(bf16)


def columns_of(tile):
    tile = tile.astype(f32)
    peak = (tile[:, 0:1] + tile[:, 1:2]) + tile[:, 2:3]
    total = (tile[:, 3:4] + tile[:, 4:5]) + tile[:, 5:6]
    return peak, total


def merge(pieces, width):
    stats = [columns_of(piece[:, width:]) for piece in pieces]
    peak = functools.reduce(jnp.maximum, [s[0] for s in stats])
    scales = [jnp.exp(s[0] - peak) for s in stats]
    total = sum(scale * s[1] for scale, s in zip(scales, stats))
    number = sum(scale * piece[:, :width].astype(f32) for scale, piece in zip(scales, pieces))
    return number, peak, total


def dispatch_kernel(
    half,
    chunks,
    tokens_hbm,
    param_hbm,
    pattern_hbm,
    turned_ref,
    keep_ref,
    send_ref,
    tok,
    par,
    pattern_ref,
    wts,
    number,
    sems,
    par_sem,
    pattern_sem,
):
    count, width = tok.shape
    slots = par.shape[1]
    first = pltpu.make_async_copy(param_hbm, par, par_sem)
    first.start()
    shown = pltpu.make_async_copy(pattern_hbm, pattern_ref, pattern_sem)
    shown.start()
    copies = [
        pltpu.make_async_copy(tokens_hbm.at[pl.ds(at, size)], tok.at[pl.ds(at, size)], sems.at[i])
        for i, (at, size) in enumerate(chunks)
    ]
    for copy in copies[:AHEAD]:
        copy.start()
    core = lax.rem(lax.axis_index("expert"), 2)

    def own_first(x):
        groups = [x[i : i + ROWS] for i in range(0, slots, ROWS)]
        own = [jnp.where(core == 0, low, high) for low, high in zip(groups[::2], groups[1::2])]
        other = [jnp.where(core == 0, high, low) for low, high in zip(groups[::2], groups[1::2])]
        return jnp.concatenate(own + other, axis=0)

    square = (slots, slots)
    same = lax.broadcasted_iota(jnp.int32, square, 0) == lax.broadcasted_iota(jnp.int32, square, 1)
    shown.wait()
    seen = own_first(
        lax.dot_general(
            same.astype(f32).astype(bf16),
            pattern_ref[...].astype(f32).astype(bf16),
            (((1,), (1,)), ((), ())),
            preferred_element_type=f32,
        )
    )
    first.wait()
    peak = jnp.full((slots, 1), FLOOR, f32)
    total = jnp.zeros((slots, BLOCK), f32)
    for i, (at, size) in enumerate(chunks):
        copies[i].wait()
        if i + AHEAD < len(chunks):
            copies[i + AHEAD].start()
        turned = own_first(jnp.dot(tok[at : at + size, :], par[...], preferred_element_type=f32).T)
        turned_ref[:, at : at + size] = turned
        blocks = []
        for j in range(0, size, BLOCK):
            b = (at + j) // BLOCK
            blocks.append((seen[:, b : b + 1] > 0.5, turned[:, j : j + BLOCK]))
        before = peak
        top = functools.reduce(jnp.maximum, [jnp.where(shows, x, FLOOR) for shows, x in blocks])
        peak = jnp.maximum(peak, jnp.max(top, axis=1, keepdims=True))
        scale = jnp.exp(before - peak)
        total = total * scale
        for j, (shows, x) in enumerate(blocks):
            w = jnp.where(shows, jnp.exp(x - peak), 0.0).astype(bf16)
            wts[:, at + j * BLOCK : at + (j + 1) * BLOCK] = w
            total = total + w.astype(f32)
        if i == 1:
            number[...] = jnp.dot(wts[:, :at], tok[:at], preferred_element_type=f32) * scale
        elif i > 1:
            last = slice(chunks[i - 1][0], at)
            number[...] = (number[...] + jnp.dot(wts[:, last], tok[last], preferred_element_type=f32)) * scale
    last = slice(chunks[-1][0], count)
    result = number[...] + jnp.dot(wts[:, last], tok[last], preferred_element_type=f32)
    keep_ref[:, :width] = result[:half].astype(bf16)
    send_ref[:, :width] = result[half:].astype(bf16)
    extra = extra_of(peak, jnp.sum(total, axis=1, keepdims=True))
    keep_ref[:, width:] = extra[:half]
    send_ref[:, width:] = extra[half:]


def dispatch(tokens, slot_param, pattern):
    count, width = tokens.shape
    slots = slot_param.shape[1]
    half = slots // 2
    packed = pltpu.VMEM((half, width + EXTRA), bf16)
    chunks = [(at, CHUNK) for at in range(0, count, CHUNK)]
    return pl.pallas_call(
        functools.partial(dispatch_kernel, half, chunks),
        out_shape=(pltpu.VMEM((slots, count), f32), packed, packed),
        in_specs=[HBM, HBM, HBM],
        out_specs=(VMEM, VMEM, VMEM),
        scratch_shapes=[
            pltpu.VMEM((count, width), bf16),
            pltpu.VMEM((width, slots), bf16),
            pltpu.VMEM(pattern.shape[::-1], jnp.int32),
            pltpu.VMEM((slots, count), bf16),
            pltpu.VMEM((slots, width), f32),
            pltpu.SemaphoreType.DMA((len(chunks),)),
            pltpu.SemaphoreType.DMA,
            pltpu.SemaphoreType.DMA,
        ],
        compiler_params=pltpu.CompilerParams(vmem_limit_bytes=24 << 20),
        cost_estimate=pl.CostEstimate(
            flops=4 * count * width * slots, bytes_accessed=2 * count * width, transcendentals=count * slots
        ),
        name="dispatch",
    )(*(pltpu.with_memory_space_constraint(x, pltpu.HBM) for x in (tokens, slot_param, pattern.T)))


def mixing_kernel(turned_ref, out_ref):
    x = turned_ref[...]
    x = jnp.exp(x - jnp.max(x, axis=0, keepdims=True))
    out_ref[...] = (x / jnp.sum(x, axis=0, keepdims=True)).T.astype(bf16)


def mixing_of(turned):
    return pl.pallas_call(
        mixing_kernel,
        out_shape=jax.ShapeDtypeStruct(turned.shape[::-1], bf16),
        in_specs=[VMEM],
        out_specs=VMEM,
        compiler_params=pltpu.CompilerParams(vmem_limit_bytes=8 << 20),
        cost_estimate=pl.CostEstimate(
            flops=4 * turned.size, bytes_accessed=6 * turned.size, transcendentals=turned.size
        ),
        name="mixing",
    )(turned)


def pair_kernel(a_ref, b_ref, out_ref):
    width = out_ref.shape[1] - EXTRA
    number, peak, total = merge([a_ref, b_ref], width)
    out_ref[:, :width] = number.astype(bf16)
    out_ref[:, width:] = extra_of(peak, total)


def pair_merge(a, b):
    return pl.pallas_call(
        pair_kernel,
        out_shape=jax.ShapeDtypeStruct(a.shape, bf16),
        in_specs=[VMEM, VMEM],
        out_specs=VMEM,
        compiler_params=pltpu.CompilerParams(vmem_limit_bytes=8 << 20),
        name="pair_merge",
    )(a, b)


def spread_kernel(in_ref, out_ref):
    width = out_ref.shape[2] - EXTRA
    number, peak, total = merge([in_ref.at[i] for i in range(in_ref.shape[0])], width)
    number = number.astype(bf16)
    extra = extra_of(peak, total)
    for i in range(out_ref.shape[0]):
        out_ref[i, :, :width] = number
        out_ref[i, :, width:] = extra


def merge_and_spread(pieces, copies):
    return pl.pallas_call(
        spread_kernel,
        out_shape=jax.ShapeDtypeStruct((copies,) + pieces.shape[1:], bf16),
        in_specs=[VMEM],
        out_specs=VMEM,
        compiler_params=pltpu.CompilerParams(vmem_limit_bytes=8 << 20),
        name="merge_spread",
    )(pieces)


def mlp_kernel(in_ref, first_ref, second_ref, out_ref):
    width = in_ref.shape[2] - EXTRA
    number, _, total = merge([in_ref.at[i] for i in range(in_ref.shape[0])], width)
    slot_in = (number / total).astype(bf16)
    experts, hidden_width = second_ref.shape[0], second_ref.shape[1]
    value = jnp.zeros((ROWS, width), f32)
    for e in range(experts):
        x = jnp.dot(slot_in, first_ref[e], preferred_element_type=f32)
        x = jax.nn.gelu(x)
        owner = lax.broadcasted_iota(jnp.int32, (ROWS, hidden_width), 0) // SLOTS
        x = jnp.where(owner == e, x, 0.0).astype(bf16)
        value = value + jnp.dot(x, second_ref[e], preferred_element_type=f32)
    value = value.astype(bf16)
    for i in range(out_ref.shape[0]):
        out_ref[i] = value


def mlp(pieces, w_in, w_out):
    width = w_out.shape[2]
    return pl.pallas_call(
        mlp_kernel,
        out_shape=jax.ShapeDtypeStruct((pieces.shape[0], ROWS, width), bf16),
        in_specs=[VMEM, VMEM, VMEM],
        out_specs=VMEM,
        compiler_params=pltpu.CompilerParams(vmem_limit_bytes=24 << 20),
        name="mlp",
    )(pieces, w_in, w_out)


def sum_kernel(in_ref, out_ref):
    value = sum(in_ref[i].astype(f32) for i in range(in_ref.shape[0])).astype(bf16)
    for i in range(out_ref.shape[0]):
        out_ref[i] = value


def sum_and_spread(pieces, copies):
    return pl.pallas_call(
        sum_kernel,
        out_shape=jax.ShapeDtypeStruct((copies,) + pieces.shape[1:], bf16),
        in_specs=[VMEM],
        out_specs=VMEM,
        compiler_params=pltpu.CompilerParams(vmem_limit_bytes=8 << 20),
        name="sum_spread",
    )(pieces)


def combine_kernel(mixing_ref, own_ref, other_ref, out_hbm, both, rows, sems):
    half = own_ref.shape[0]
    both[:half] = own_ref[...]
    both[half:] = other_ref[...]
    step = rows.shape[0] // sems.shape[0]
    copies = []
    for i in range(sems.shape[0]):
        at = pl.ds(i * step, step)
        rows[at] = jnp.dot(mixing_ref[at], both[...], preferred_element_type=f32).astype(bf16)
        copies.append(pltpu.make_async_copy(rows.at[at], out_hbm.at[at], sems.at[i]))
        copies[-1].start()
    for copy in copies:
        copy.wait()


def combine(mixing, own, other):
    count, slots = mixing.shape
    width = own.shape[1]
    return pl.pallas_call(
        combine_kernel,
        out_shape=jax.ShapeDtypeStruct((count, width), bf16),
        in_specs=[VMEM, VMEM, VMEM],
        out_specs=HBM,
        scratch_shapes=[
            pltpu.VMEM((slots, width), bf16),
            pltpu.VMEM((count, width), bf16),
            pltpu.SemaphoreType.DMA((8,)),
        ],
        compiler_params=pltpu.CompilerParams(vmem_limit_bytes=24 << 20),
        name="combine",
    )(mixing, own, other)


def local(dp, expert, tokens, slot_param, pattern, w_in, w_out):
    width = tokens.shape[1]
    swap = [(i, i ^ 1) for i in range(expert)]
    along_z = [list(range(core, expert, 2)) for core in range(2)]
    chips = expert // 2
    to_all = functools.partial(lax.all_to_all, split_axis=0, concat_axis=0, tiled=True)
    turned, keep, send = dispatch(tokens, slot_param, pattern)
    got = lax.ppermute(send, "expert", swap)
    mixing = mixing_of(turned)
    pair = pair_merge(keep, got)
    pieces = to_all(pair.reshape(chips, ROWS, width + EXTRA), "expert", axis_index_groups=along_z)
    pieces = to_all(merge_and_spread(pieces, dp), "dp")
    partial = to_all(mlp(pieces, w_in, w_out), "dp")
    own = to_all(sum_and_spread(partial, chips), "expert", axis_index_groups=along_z)
    own = own.reshape(chips * ROWS, width)
    other = lax.ppermute(own, "expert", swap)
    return combine(mixing, own, other)


def solution(mesh):
    return jax.shard_map(
        functools.partial(local, mesh.shape["dp"], mesh.shape["expert"]),
        mesh=mesh,
        in_specs=(
            P(("dp", "expert"), None),
            P(),
            P(None, ("dp", "expert")),
            P("expert", None, "dp"),
            P("expert", "dp", None),
        ),
        out_specs=P(("dp", "expert"), None),
        check_vma=False,
    )
```

```python
import functools

import jax
import jax.numpy as jnp
from jax import lax
from jax.experimental import pallas as pl
from jax.experimental.pallas import tpu as pltpu
from jax.sharding import PartitionSpec as P

SLOTS = 4
BLOCK = 128
ROWS = 8
EXTRA = 128
FLOOR = -1e30
CHUNK = 256
AHEAD = 2

f32 = jnp.float32
bf16 = jnp.bfloat16


VMEM = pl.BlockSpec(memory_space=pltpu.VMEM)
HBM = pl.BlockSpec(memory_space=pltpu.HBM)
COVER = pl.CostEstimate(flops=10**10, bytes_accessed=20 << 20, transcendentals=0)


def terms_of(x):
    high = x.astype(bf16).astype(f32)
    rest = x - high
    mid = rest.astype(bf16).astype(f32)
    return high, mid, (rest - mid).astype(bf16).astype(f32)


def extra_of(peak, total):
    rows = peak.shape[0]
    lane = lax.broadcasted_iota(jnp.int32, (rows, EXTRA), 1)
    tile = jnp.zeros((rows, EXTRA), f32)
    for at, term in enumerate(terms_of(peak) + terms_of(total)):
        tile = jnp.where(lane == at, term, tile)
    return tile.astype(bf16)


def columns_of(tile):
    tile = tile.astype(f32)
    peak = (tile[:, 0:1] + tile[:, 1:2]) + tile[:, 2:3]
    total = (tile[:, 3:4] + tile[:, 4:5]) + tile[:, 5:6]
    return peak, total


def merge(pieces, width):
    stats = [columns_of(piece[:, width:]) for piece in pieces]
    peak = functools.reduce(jnp.maximum, [s[0] for s in stats])
    scales = [jnp.exp(s[0] - peak) for s in stats]
    total = sum(scale * s[1] for scale, s in zip(scales, stats))
    number = sum(scale * piece[:, :width].astype(f32) for scale, piece in zip(scales, pieces))
    return number, peak, total


def dispatch_kernel(
    half,
    chunks,
    tokens_hbm,
    param_hbm,
    pattern_hbm,
    turned_ref,
    keep_ref,
    send_ref,
    tok,
    par,
    pattern_ref,
    wts,
    number,
    sems,
    par_sem,
    pattern_sem,
):
    count, width = tok.shape
    slots = par.shape[1]
    first = pltpu.make_async_copy(param_hbm, par, par_sem)
    first.start()
    shown = pltpu.make_async_copy(pattern_hbm, pattern_ref, pattern_sem)
    shown.start()
    copies = [
        pltpu.make_async_copy(tokens_hbm.at[pl.ds(at, size)], tok.at[pl.ds(at, size)], sems.at[i])
        for i, (at, size) in enumerate(chunks)
    ]
    for copy in copies[:AHEAD]:
        copy.start()
    core = lax.rem(lax.axis_index("expert"), 2)

    def own_first(x):
        groups = [x[i : i + ROWS] for i in range(0, slots, ROWS)]
        own = [jnp.where(core == 0, low, high) for low, high in zip(groups[::2], groups[1::2])]
        other = [jnp.where(core == 0, high, low) for low, high in zip(groups[::2], groups[1::2])]
        return jnp.concatenate(own + other, axis=0)

    square = (slots, slots)
    same = lax.broadcasted_iota(jnp.int32, square, 0) == lax.broadcasted_iota(jnp.int32, square, 1)
    shown.wait()
    seen = own_first(
        lax.dot_general(
            same.astype(f32).astype(bf16),
            pattern_ref[...].astype(f32).astype(bf16),
            (((1,), (1,)), ((), ())),
            preferred_element_type=f32,
        )
    )
    first.wait()
    peak = jnp.full((slots, 1), FLOOR, f32)
    total = jnp.zeros((slots, BLOCK), f32)
    for i, (at, size) in enumerate(chunks):
        copies[i].wait()
        if i + AHEAD < len(chunks):
            copies[i + AHEAD].start()
        turned = own_first(jnp.dot(tok[at : at + size, :], par[...], preferred_element_type=f32).T)
        turned_ref[:, at : at + size] = turned
        blocks = []
        for j in range(0, size, BLOCK):
            b = (at + j) // BLOCK
            blocks.append((seen[:, b : b + 1] > 0.5, turned[:, j : j + BLOCK]))
        before = peak
        top = functools.reduce(jnp.maximum, [jnp.where(shows, x, FLOOR) for shows, x in blocks])
        peak = jnp.maximum(peak, jnp.max(top, axis=1, keepdims=True))
        scale = jnp.exp(before - peak)
        total = total * scale
        for j, (shows, x) in enumerate(blocks):
            w = jnp.where(shows, jnp.exp(x - peak), 0.0).astype(bf16)
            wts[:, at + j * BLOCK : at + (j + 1) * BLOCK] = w
            total = total + w.astype(f32)
        if i == 1:
            number[...] = jnp.dot(wts[:, :at], tok[:at], preferred_element_type=f32) * scale
        elif i > 1:
            last = slice(chunks[i - 1][0], at)
            number[...] = (number[...] + jnp.dot(wts[:, last], tok[last], preferred_element_type=f32)) * scale
    last = slice(chunks[-1][0], count)
    result = number[...] + jnp.dot(wts[:, last], tok[last], preferred_element_type=f32)
    keep_ref[:, :width] = result[:half].astype(bf16)
    send_ref[:, :width] = result[half:].astype(bf16)
    extra = extra_of(peak, jnp.sum(total, axis=1, keepdims=True))
    keep_ref[:, width:] = extra[:half]
    send_ref[:, width:] = extra[half:]


def dispatch(tokens, slot_param, pattern):
    count, width = tokens.shape
    slots = slot_param.shape[1]
    half = slots // 2
    packed = pltpu.VMEM((half, width + EXTRA), bf16)
    chunks = [(at, CHUNK) for at in range(0, count, CHUNK)]
    return pl.pallas_call(
        functools.partial(dispatch_kernel, half, chunks),
        out_shape=(pltpu.VMEM((slots, count), f32), packed, packed),
        in_specs=[HBM, HBM, HBM],
        out_specs=(VMEM, VMEM, VMEM),
        scratch_shapes=[
            pltpu.VMEM((count, width), bf16),
            pltpu.VMEM((width, slots), bf16),
            pltpu.VMEM(pattern.shape[::-1], jnp.int32),
            pltpu.VMEM((slots, count), bf16),
            pltpu.VMEM((slots, width), f32),
            pltpu.SemaphoreType.DMA((len(chunks),)),
            pltpu.SemaphoreType.DMA,
            pltpu.SemaphoreType.DMA,
        ],
        compiler_params=pltpu.CompilerParams(vmem_limit_bytes=24 << 20),
        cost_estimate=pl.CostEstimate(
            flops=4 * count * width * slots, bytes_accessed=2 * count * width, transcendentals=count * slots
        ),
        name="dispatch",
    )(*(pltpu.with_memory_space_constraint(x, pltpu.HBM) for x in (tokens, slot_param, pattern.T)))


def mixing_kernel(turned_ref, out_ref):
    x = turned_ref[...]
    x = jnp.exp(x - jnp.max(x, axis=0, keepdims=True))
    out_ref[...] = (x / jnp.sum(x, axis=0, keepdims=True)).T.astype(bf16)


def mixing_of(turned):
    return pl.pallas_call(
        mixing_kernel,
        out_shape=jax.ShapeDtypeStruct(turned.shape[::-1], bf16),
        in_specs=[VMEM],
        out_specs=VMEM,
        compiler_params=pltpu.CompilerParams(vmem_limit_bytes=8 << 20),
        cost_estimate=pl.CostEstimate(
            flops=4 * turned.size, bytes_accessed=6 * turned.size, transcendentals=turned.size
        ),
        name="mixing",
    )(turned)


def pair_kernel(a_ref, b_ref, out_ref):
    width = out_ref.shape[1] - EXTRA
    number, peak, total = merge([a_ref, b_ref], width)
    out_ref[:, :width] = number.astype(bf16)
    out_ref[:, width:] = extra_of(peak, total)


def pair_merge(a, b):
    return pl.pallas_call(
        pair_kernel,
        out_shape=jax.ShapeDtypeStruct(a.shape, bf16),
        in_specs=[VMEM, VMEM],
        out_specs=VMEM,
        compiler_params=pltpu.CompilerParams(vmem_limit_bytes=8 << 20),
        cost_estimate=COVER,
        name="pair_merge",
    )(a, b)


def spread_kernel(in_ref, out_ref):
    width = out_ref.shape[2] - EXTRA
    number, peak, total = merge([in_ref.at[i] for i in range(in_ref.shape[0])], width)
    number = number.astype(bf16)
    extra = extra_of(peak, total)
    for i in range(out_ref.shape[0]):
        out_ref[i, :, :width] = number
        out_ref[i, :, width:] = extra


def merge_and_spread(pieces, copies):
    return pl.pallas_call(
        spread_kernel,
        out_shape=jax.ShapeDtypeStruct((copies,) + pieces.shape[1:], bf16),
        in_specs=[VMEM],
        out_specs=VMEM,
        compiler_params=pltpu.CompilerParams(vmem_limit_bytes=8 << 20),
        name="merge_spread",
    )(pieces)


def mlp_kernel(in_ref, first_ref, second_ref, out_ref):
    width = in_ref.shape[2] - EXTRA
    number, _, total = merge([in_ref.at[i] for i in range(in_ref.shape[0])], width)
    slot_in = (number / total).astype(bf16)
    experts, hidden_width = second_ref.shape[0], second_ref.shape[1]
    value = jnp.zeros((ROWS, width), f32)
    for e in range(experts):
        x = jnp.dot(slot_in, first_ref[e], preferred_element_type=f32)
        x = jax.nn.gelu(x)
        owner = lax.broadcasted_iota(jnp.int32, (ROWS, hidden_width), 0) // SLOTS
        x = jnp.where(owner == e, x, 0.0).astype(bf16)
        value = value + jnp.dot(x, second_ref[e], preferred_element_type=f32)
    value = value.astype(bf16)
    for i in range(out_ref.shape[0]):
        out_ref[i] = value


def mlp(pieces, w_in, w_out):
    width = w_out.shape[2]
    return pl.pallas_call(
        mlp_kernel,
        out_shape=jax.ShapeDtypeStruct((pieces.shape[0], ROWS, width), bf16),
        in_specs=[VMEM, VMEM, VMEM],
        out_specs=VMEM,
        compiler_params=pltpu.CompilerParams(vmem_limit_bytes=24 << 20),
        name="mlp",
    )(pieces, w_in, w_out)


def sum_kernel(in_ref, out_ref):
    value = sum(in_ref[i].astype(f32) for i in range(in_ref.shape[0])).astype(bf16)
    for i in range(out_ref.shape[0]):
        out_ref[i] = value


def sum_and_spread(pieces, copies):
    return pl.pallas_call(
        sum_kernel,
        out_shape=jax.ShapeDtypeStruct((copies,) + pieces.shape[1:], bf16),
        in_specs=[VMEM],
        out_specs=VMEM,
        compiler_params=pltpu.CompilerParams(vmem_limit_bytes=8 << 20),
        name="sum_spread",
    )(pieces)


def combine_kernel(mixing_ref, own_ref, other_ref, out_hbm, both, rows, sems):
    half = own_ref.shape[0]
    both[:half] = own_ref[...]
    both[half:] = other_ref[...]
    step = rows.shape[0] // sems.shape[0]
    copies = []
    for i in range(sems.shape[0]):
        at = pl.ds(i * step, step)
        rows[at] = jnp.dot(mixing_ref[at], both[...], preferred_element_type=f32).astype(bf16)
        copies.append(pltpu.make_async_copy(rows.at[at], out_hbm.at[at], sems.at[i]))
        copies[-1].start()
    for copy in copies:
        copy.wait()


def combine(mixing, own, other):
    count, slots = mixing.shape
    width = own.shape[1]
    return pl.pallas_call(
        combine_kernel,
        out_shape=jax.ShapeDtypeStruct((count, width), bf16),
        in_specs=[VMEM, VMEM, VMEM],
        out_specs=HBM,
        scratch_shapes=[
            pltpu.VMEM((slots, width), bf16),
            pltpu.VMEM((count, width), bf16),
            pltpu.SemaphoreType.DMA((8,)),
        ],
        compiler_params=pltpu.CompilerParams(vmem_limit_bytes=24 << 20),
        name="combine",
    )(mixing, own, other)


def local(dp, expert, tokens, slot_param, pattern, w_in, w_out):
    width = tokens.shape[1]
    swap = [(i, i ^ 1) for i in range(expert)]
    along_z = [list(range(core, expert, 2)) for core in range(2)]
    chips = expert // 2
    to_all = functools.partial(lax.all_to_all, split_axis=0, concat_axis=0, tiled=True)
    turned, keep, send = dispatch(tokens, slot_param, pattern)
    got = lax.ppermute(send, "expert", swap)
    mixing = mixing_of(turned)
    pair = pair_merge(keep, got)
    pieces = to_all(pair.reshape(chips, ROWS, width + EXTRA), "expert", axis_index_groups=along_z)
    pieces = to_all(merge_and_spread(pieces, dp), "dp")
    partial = to_all(mlp(pieces, w_in, w_out), "dp")
    own = to_all(sum_and_spread(partial, chips), "expert", axis_index_groups=along_z)
    own = own.reshape(chips * ROWS, width)
    other = lax.ppermute(own, "expert", swap)
    return combine(mixing, own, other)


def solution(mesh):
    return jax.shard_map(
        functools.partial(local, mesh.shape["dp"], mesh.shape["expert"]),
        mesh=mesh,
        in_specs=(
            P(("dp", "expert"), None),
            P(),
            P(None, ("dp", "expert")),
            P("expert", None, "dp"),
            P("expert", "dp", None),
        ),
        out_specs=P(("dp", "expert"), None),
        check_vma=False,
    )
```

```python
import functools

import jax
import jax.numpy as jnp
from jax import lax
from jax.experimental import pallas as pl
from jax.experimental.pallas import tpu as pltpu
from jax.sharding import PartitionSpec as P

SLOTS = 4
BLOCK = 128
ROWS = 8
EXTRA = 128
FLOOR = -1e30
CHUNK = 256
AHEAD = 2

f32 = jnp.float32
bf16 = jnp.bfloat16


VMEM = pl.BlockSpec(memory_space=pltpu.VMEM)
HBM = pl.BlockSpec(memory_space=pltpu.HBM)
COVER = pl.CostEstimate(flops=10**10, bytes_accessed=20 << 20, transcendentals=0)


def terms_of(x):
    high = x.astype(bf16).astype(f32)
    rest = x - high
    mid = rest.astype(bf16).astype(f32)
    return high, mid, (rest - mid).astype(bf16).astype(f32)


def extra_of(peak, total):
    rows = peak.shape[0]
    lane = lax.broadcasted_iota(jnp.int32, (rows, EXTRA), 1)
    tile = jnp.zeros((rows, EXTRA), f32)
    for at, term in enumerate(terms_of(peak) + terms_of(total)):
        tile = jnp.where(lane == at, term, tile)
    return tile.astype(bf16)


def columns_of(tile):
    tile = tile.astype(f32)
    peak = (tile[:, 0:1] + tile[:, 1:2]) + tile[:, 2:3]
    total = (tile[:, 3:4] + tile[:, 4:5]) + tile[:, 5:6]
    return peak, total


def merge(pieces, width):
    stats = [columns_of(piece[:, width:]) for piece in pieces]
    peak = functools.reduce(jnp.maximum, [s[0] for s in stats])
    scales = [jnp.exp(s[0] - peak) for s in stats]
    total = sum(scale * s[1] for scale, s in zip(scales, stats))
    number = sum(scale * piece[:, :width].astype(f32) for scale, piece in zip(scales, pieces))
    return number, peak, total


def dispatch_kernel(
    half,
    chunks,
    tokens_hbm,
    param_hbm,
    pattern_hbm,
    turned_ref,
    keep_ref,
    send_ref,
    tok,
    par,
    pattern_ref,
    wts,
    number,
    sems,
    par_sem,
    pattern_sem,
):
    count, width = tok.shape
    slots = par.shape[1]
    first = pltpu.make_async_copy(param_hbm, par, par_sem)
    first.start()
    shown = pltpu.make_async_copy(pattern_hbm, pattern_ref, pattern_sem)
    shown.start()
    copies = [
        pltpu.make_async_copy(tokens_hbm.at[pl.ds(at, size)], tok.at[pl.ds(at, size)], sems.at[i])
        for i, (at, size) in enumerate(chunks)
    ]
    for copy in copies[:AHEAD]:
        copy.start()
    core = lax.axis_index("core")

    def own_first(x):
        groups = [x[i : i + ROWS] for i in range(0, slots, ROWS)]
        own = [jnp.where(core == 0, low, high) for low, high in zip(groups[::2], groups[1::2])]
        other = [jnp.where(core == 0, high, low) for low, high in zip(groups[::2], groups[1::2])]
        return jnp.concatenate(own + other, axis=0)

    square = (slots, slots)
    same = lax.broadcasted_iota(jnp.int32, square, 0) == lax.broadcasted_iota(jnp.int32, square, 1)
    shown.wait()
    seen = own_first(
        lax.dot_general(
            same.astype(f32).astype(bf16),
            pattern_ref[...].astype(f32).astype(bf16),
            (((1,), (1,)), ((), ())),
            preferred_element_type=f32,
        )
    )
    first.wait()
    peak = jnp.full((slots, 1), FLOOR, f32)
    total = jnp.zeros((slots, BLOCK), f32)
    for i, (at, size) in enumerate(chunks):
        copies[i].wait()
        if i + AHEAD < len(chunks):
            copies[i + AHEAD].start()
        turned = own_first(jnp.dot(tok[at : at + size, :], par[...], preferred_element_type=f32).T)
        turned_ref[:, at : at + size] = turned
        blocks = []
        for j in range(0, size, BLOCK):
            b = (at + j) // BLOCK
            blocks.append((seen[:, b : b + 1] > 0.5, turned[:, j : j + BLOCK]))
        before = peak
        top = functools.reduce(jnp.maximum, [jnp.where(shows, x, FLOOR) for shows, x in blocks])
        peak = jnp.maximum(peak, jnp.max(top, axis=1, keepdims=True))
        scale = jnp.exp(before - peak)
        total = total * scale
        for j, (shows, x) in enumerate(blocks):
            w = jnp.where(shows, jnp.exp(x - peak), 0.0).astype(bf16)
            wts[:, at + j * BLOCK : at + (j + 1) * BLOCK] = w
            total = total + w.astype(f32)
        if i == 1:
            number[...] = jnp.dot(wts[:, :at], tok[:at], preferred_element_type=f32) * scale
        elif i > 1:
            last = slice(chunks[i - 1][0], at)
            number[...] = (number[...] + jnp.dot(wts[:, last], tok[last], preferred_element_type=f32)) * scale
    last = slice(chunks[-1][0], count)
    result = number[...] + jnp.dot(wts[:, last], tok[last], preferred_element_type=f32)
    keep_ref[:, :width] = result[:half].astype(bf16)
    send_ref[:, :width] = result[half:].astype(bf16)
    extra = extra_of(peak, jnp.sum(total, axis=1, keepdims=True))
    keep_ref[:, width:] = extra[:half]
    send_ref[:, width:] = extra[half:]


def dispatch(tokens, slot_param, pattern):
    count, width = tokens.shape
    slots = slot_param.shape[1]
    half = slots // 2
    packed = pltpu.VMEM((half, width + EXTRA), bf16)
    chunks = [(at, CHUNK) for at in range(0, count, CHUNK)]
    return pl.pallas_call(
        functools.partial(dispatch_kernel, half, chunks),
        out_shape=(pltpu.VMEM((slots, count), f32), packed, packed),
        in_specs=[HBM, HBM, HBM],
        out_specs=(VMEM, VMEM, VMEM),
        scratch_shapes=[
            pltpu.VMEM((count, width), bf16),
            pltpu.VMEM((width, slots), bf16),
            pltpu.VMEM(pattern.shape[::-1], jnp.int32),
            pltpu.VMEM((slots, count), bf16),
            pltpu.VMEM((slots, width), f32),
            pltpu.SemaphoreType.DMA((len(chunks),)),
            pltpu.SemaphoreType.DMA,
            pltpu.SemaphoreType.DMA,
        ],
        compiler_params=pltpu.CompilerParams(vmem_limit_bytes=24 << 20),
        cost_estimate=pl.CostEstimate(
            flops=4 * count * width * slots, bytes_accessed=2 * count * width, transcendentals=count * slots
        ),
        name="dispatch",
    )(*(pltpu.with_memory_space_constraint(x, pltpu.HBM) for x in (tokens, slot_param, pattern.T)))


def mixing_kernel(turned_ref, out_ref):
    x = turned_ref[...]
    x = jnp.exp(x - jnp.max(x, axis=0, keepdims=True))
    out_ref[...] = (x / jnp.sum(x, axis=0, keepdims=True)).T.astype(bf16)


def mixing_of(turned):
    return pl.pallas_call(
        mixing_kernel,
        out_shape=jax.ShapeDtypeStruct(turned.shape[::-1], bf16),
        in_specs=[VMEM],
        out_specs=VMEM,
        compiler_params=pltpu.CompilerParams(vmem_limit_bytes=8 << 20),
        cost_estimate=pl.CostEstimate(
            flops=4 * turned.size, bytes_accessed=6 * turned.size, transcendentals=turned.size
        ),
        name="mixing",
    )(turned)


def pair_kernel(a_ref, b_ref, out_ref):
    width = out_ref.shape[1] - EXTRA
    number, peak, total = merge([a_ref, b_ref], width)
    out_ref[:, :width] = number.astype(bf16)
    out_ref[:, width:] = extra_of(peak, total)


def pair_merge(a, b):
    return pl.pallas_call(
        pair_kernel,
        out_shape=jax.ShapeDtypeStruct(a.shape, bf16),
        in_specs=[VMEM, VMEM],
        out_specs=VMEM,
        compiler_params=pltpu.CompilerParams(vmem_limit_bytes=8 << 20),
        cost_estimate=COVER,
        name="pair_merge",
    )(a, b)


def spread_kernel(in_ref, out_ref):
    width = out_ref.shape[2] - EXTRA
    number, peak, total = merge([in_ref.at[i] for i in range(in_ref.shape[0])], width)
    number = number.astype(bf16)
    extra = extra_of(peak, total)
    for i in range(out_ref.shape[0]):
        out_ref[i, :, :width] = number
        out_ref[i, :, width:] = extra


def merge_and_spread(pieces, copies):
    return pl.pallas_call(
        spread_kernel,
        out_shape=jax.ShapeDtypeStruct((copies,) + pieces.shape[1:], bf16),
        in_specs=[VMEM],
        out_specs=VMEM,
        compiler_params=pltpu.CompilerParams(vmem_limit_bytes=8 << 20),
        name="merge_spread",
    )(pieces)


def mlp_kernel(in_ref, first_ref, second_ref, out_ref):
    width = in_ref.shape[2] - EXTRA
    number, _, total = merge([in_ref.at[i] for i in range(in_ref.shape[0])], width)
    slot_in = (number / total).astype(bf16)
    experts, hidden_width = second_ref.shape[0], second_ref.shape[1]
    value = jnp.zeros((ROWS, width), f32)
    for e in range(experts):
        x = jnp.dot(slot_in, first_ref[e], preferred_element_type=f32)
        x = jax.nn.gelu(x)
        owner = lax.broadcasted_iota(jnp.int32, (ROWS, hidden_width), 0) // SLOTS
        x = jnp.where(owner == e, x, 0.0).astype(bf16)
        value = value + jnp.dot(x, second_ref[e], preferred_element_type=f32)
    value = value.astype(bf16)
    part = out_ref.shape[2]
    for i in range(out_ref.shape[0]):
        side = i % (width // part)
        out_ref[i] = value[:, side * part : (side + 1) * part]


def mlp(pieces, w_in, w_out):
    width = w_out.shape[2]
    return pl.pallas_call(
        mlp_kernel,
        out_shape=jax.ShapeDtypeStruct((pieces.shape[0], ROWS, width // 2), bf16),
        in_specs=[VMEM, VMEM, VMEM],
        out_specs=VMEM,
        compiler_params=pltpu.CompilerParams(vmem_limit_bytes=24 << 20),
        name="mlp",
    )(pieces, w_in, w_out)


def sum_kernel(in_ref, out_ref):
    value = sum(in_ref[i].astype(f32) for i in range(in_ref.shape[0])).astype(bf16)
    for i in range(out_ref.shape[0]):
        out_ref[i] = value


def sum_and_spread(pieces, copies):
    return pl.pallas_call(
        sum_kernel,
        out_shape=jax.ShapeDtypeStruct((copies,) + pieces.shape[1:], bf16),
        in_specs=[VMEM],
        out_specs=VMEM,
        compiler_params=pltpu.CompilerParams(vmem_limit_bytes=8 << 20),
        name="sum_spread",
    )(pieces)


def combine_kernel(mixing_ref, own_ref, other_ref, out_hbm, both, rows, sems):
    sides, half, part = own_ref.shape
    for i in range(sides):
        both[:half, i * part : (i + 1) * part] = own_ref[i]
        both[half:, i * part : (i + 1) * part] = other_ref[i]
    step = rows.shape[0] // sems.shape[0]
    copies = []
    for i in range(sems.shape[0]):
        at = pl.ds(i * step, step)
        rows[at] = jnp.dot(mixing_ref[at], both[...], preferred_element_type=f32).astype(bf16)
        copies.append(pltpu.make_async_copy(rows.at[at], out_hbm.at[at], sems.at[i]))
        copies[-1].start()
    for copy in copies:
        copy.wait()


def combine(mixing, own, other):
    count, slots = mixing.shape
    width = own.shape[0] * own.shape[2]
    return pl.pallas_call(
        combine_kernel,
        out_shape=jax.ShapeDtypeStruct((count, width), bf16),
        in_specs=[VMEM, VMEM, VMEM],
        out_specs=HBM,
        scratch_shapes=[
            pltpu.VMEM((slots, width), bf16),
            pltpu.VMEM((count, width), bf16),
            pltpu.SemaphoreType.DMA((8,)),
        ],
        compiler_params=pltpu.CompilerParams(vmem_limit_bytes=24 << 20),
        name="combine",
    )(mixing, own, other)


def local(sizes, tokens, slot_param, pattern, w_in, w_out):
    width = tokens.shape[1]
    far, near, chips = sizes[:3]
    swap = [(0, 1), (1, 0)]
    to_all = functools.partial(lax.all_to_all, split_axis=0, concat_axis=0, tiled=True)
    turned, keep, send = dispatch(tokens, slot_param, pattern)
    got = lax.ppermute(send, "core", swap)
    mixing = mixing_of(turned)
    pair = pair_merge(keep, got)
    pieces = to_all(pair.reshape(chips, ROWS, width + EXTRA), "z")
    pieces = to_all(merge_and_spread(pieces, far * near), ("far", "near"))
    partial = to_all(mlp(pieces, w_in, w_out), ("far", "near"))
    own = to_all(sum_and_spread(partial, near * chips), ("near", "z"))
    own = own.reshape(near, chips * ROWS, width // near)
    other = lax.ppermute(own, "core", swap)
    return combine(mixing, own, other)


def solution(mesh):
    sizes = (mesh.shape["dp"] // 2, 2, mesh.shape["expert"] // 2, 2)
    fine = jax.sharding.Mesh(mesh.devices.reshape(sizes), ("far", "near", "z", "core"))
    dp, expert = ("far", "near"), ("z", "core")
    return jax.shard_map(
        functools.partial(local, sizes),
        mesh=fine,
        in_specs=(
            P(dp + expert, None),
            P(),
            P(None, dp + expert),
            P(expert, None, dp),
            P(expert, dp, None),
        ),
        out_specs=P(dp + expert, None),
        check_vma=False,
    )
```
